32 devices in a mesh: groups: 2 (over y), rows: 4 (over x, core), cols: 4 (over z).
Axes of the slice: x: 2, y: 2, z: 4, core: 2. Of those that a mesh axis runs over, the one named last changes fastest.
Arguments:
- pair_rep: float32 [384, 192, 128], P(('groups', 'cols'), 'rows'), parts along dimension 0, may hold values from -6 to 6
- token_mask: int32 [384], P(('groups', 'rows')), parts along dimension 0, may hold values from 0 to 1, as said below
- norm_gain: float32 [128], replicated, may hold values from 0.1 to 1.9
- norm_shift: float32 [128], replicated, may hold values from -3 to 3
- w_query: bfloat16 [128, 128], replicated, may hold values from -0.5 to 0.5
- w_keyval: bfloat16 [128, 256], replicated, may hold values from -0.5 to 0.5
- w_gate: bfloat16 [128, 128], replicated, may hold values from -0.5 to 0.5
- gate_shift: float32 [128], replicated, may hold values from -3 to 3
- w_bias: float32 [128, 4], replicated, may hold values from -12 to 12
- w_out: bfloat16 [128, 128], replicated, may hold values from -0.5 to 0.5
- out_shift: float32 [128], replicated, may hold values from -3 to 3
Outputs:
- pair_update: float32 [384, 192, 128], P(('groups', 'cols'), 'rows'), parts along dimension 0
The draws below stay inside these ranges and needn't reach their ends.
There are 2 independent parts, one for each index of `groups`. The reference program is written for one: setup_inputs(seed, part) draws one part's arguments, and reference() takes and returns one part's arrays. A program takes and returns all parts, laid end to end along the dimension named above; an argument that names none is the same for every part. Nothing has to cross between parts.
Inputs may be any that keep to these rules, and one draw needn't show every extreme that they name: `token_mask`: position 0 is always a valid residue and the last position never is.
All inputs are finite; a program needn't handle non-finite values.
Results may differ from the reference program's by a relative error of at most 0.012.
The reference program's roundings to bfloat16 on the way (of `normed`, `queries`, `keyvals`, `weights` and `gated`) count: a program that leaves them out, or rounds other values in their place, can miss the bound.
Values may be sent and summed in bfloat16 or wider, within the bound.
No kernel may reach another device: no remote copies, remote signals or barrier semaphores. Data moves between devices by JAX's collectives and lax.ppermute only.
A program may use at most 128 MiB of HBM per device.

```python
import math
import jax
import jax.numpy as jnp
from jax import lax

C = 128
HEADS = 4
HEAD_DIM = 32
TOKENS = 192


def draw_token_mask(key, part):
    first_key, second_key = jax.random.split(jax.random.fold_in(key, 11))
    length = jax.random.randint(first_key, (), TOKENS // 2, TOKENS + 1)
    gap_draws = jax.random.randint(second_key, (TOKENS,), 0, 10)
    positions = jnp.arange(TOKENS)
    usable = (positions < length) & (gap_draws != 0)
    usable = jnp.where(positions == 0, True, usable)
    usable = jnp.where(positions == TOKENS - 1, False, usable)
    return usable.astype(jnp.int32)


def draw_w_bias(key, part):
    spread = 3.0
    values = jax.random.normal(jax.random.fold_in(key, 23), (C, HEADS), jnp.float32) * spread / math.sqrt(C)
    return jnp.clip(values, -12.0, 12.0)


def levels(key, shape, cuts, low, top_value):
    level, own = 1.0, jax.random.fold_in(key, 6)
    for axis_at, shards_of in cuts:
        draws = jnp.exp(jax.random.uniform(jax.random.fold_in(own, axis_at), (shards_of,), jnp.float32, low / len(cuts), top_value / len(cuts)))
        level = level * jnp.repeat(draws, shape[axis_at] // shards_of).reshape([-1 if axis == axis_at else 1 for axis in range(len(shape))])
    return level


def scatter_about(own_key, dims, scale, reach, cuts=(), kind=jnp.bfloat16):
    drawn = scale * jax.random.normal(own_key, dims, jnp.float32)
    if cuts:
        drawn = drawn * levels(own_key, dims, cuts, -0.22, 0.18)
    return jnp.clip(drawn, -reach, reach).astype(kind)


def setup_inputs(seed: int = 0, part: int = 0) -> dict:
    arg_keys = jax.random.split(jax.random.key(seed), 12)
    own_keys = jax.random.split(jax.random.fold_in(arg_keys[11], part), 12)
    return {
        "pair_rep": scatter_about(own_keys[0], (TOKENS, TOKENS, C), 1.0, 6.0, ((0, 4), (1, 4)), jnp.float32),
        "token_mask": draw_token_mask(jax.random.fold_in(jax.random.fold_in(arg_keys[11], part), 71), part),
        "norm_gain": jnp.clip(1.0 + 0.18 * jax.random.normal(arg_keys[2], (C,), jnp.float32), 0.1, 1.9),
        "norm_shift": scatter_about(arg_keys[3], (C,), 0.5, 3.0, (), jnp.float32),
        "w_query": scatter_about(arg_keys[4], (C, C), C ** -0.5, 0.5),
        "w_keyval": scatter_about(arg_keys[5], (C, 2 * C), C ** -0.5, 0.5),
        "w_gate": scatter_about(arg_keys[6], (C, C), C ** -0.5, 0.5),
        "gate_shift": scatter_about(arg_keys[7], (C,), 1.0, 3.0, (), jnp.float32),
        "w_bias": draw_w_bias(jax.random.fold_in(arg_keys[11], 71), part),
        "w_out": scatter_about(arg_keys[9], (C, C), C ** -0.5, 0.5),
        "out_shift": scatter_about(arg_keys[10], (C,), 0.5, 3.0, (), jnp.float32),
    }


def layer_norm(values, norm_gain, norm_shift):
    mean_val = lax.optimization_barrier(jnp.mean(values, axis=-1, keepdims=True))
    centred = values - mean_val
    variance = lax.optimization_barrier(jnp.mean(centred * centred, axis=-1, keepdims=True))
    return (centred * lax.rsqrt(variance + 1e-05) * norm_gain + norm_shift).astype(jnp.bfloat16)

def reference(pair_rep, token_mask, norm_gain, norm_shift, w_query, w_keyval, w_gate, gate_shift, w_bias, w_out, out_shift):
    normed = layer_norm(pair_rep, norm_gain, norm_shift)
    queries = (jnp.dot(normed, w_query, preferred_element_type=jnp.float32) * HEAD_DIM ** (-0.5)).astype(jnp.bfloat16)
    keyvals = jnp.dot(normed, w_keyval, preferred_element_type=jnp.float32).astype(jnp.bfloat16)
    gates = jax.nn.sigmoid(jnp.dot(normed, w_gate, preferred_element_type=jnp.float32) + gate_shift)
    tri_bias = jnp.dot(normed.astype(jnp.float32), w_bias, precision=lax.Precision.HIGHEST).transpose(2, 0, 1)
    usable = token_mask > 0
    group_rows = 4
    query_blocks = queries.reshape(TOKENS // group_rows, group_rows, TOKENS, HEADS, HEAD_DIM)
    keyval_blocks = keyvals.reshape(TOKENS // group_rows, group_rows, TOKENS, 2 * C)
    gate_blocks = gates.reshape(TOKENS // group_rows, group_rows, TOKENS, C)

    def one_block(operands):
        query_part, keyval_part, gate_part = operands
        keys = keyval_part[..., :C].reshape(group_rows, TOKENS, HEADS, HEAD_DIM)
        values = keyval_part[..., C:].reshape(group_rows, TOKENS, HEADS, HEAD_DIM)
        scores = jnp.einsum('ijhd,ikhd->hijk', query_part.astype(jnp.float32), keys.astype(jnp.float32))
        scores = scores + tri_bias[:, None]
        scores = jnp.where(usable[None, None, None, :], scores, jnp.float32(-1000000000.0))
        highest = lax.optimization_barrier(jnp.max(scores, axis=-1, keepdims=True))
        expo = jnp.exp(scores - highest)
        total = lax.optimization_barrier(jnp.sum(expo, axis=-1))
        weights = expo.astype(jnp.bfloat16)
        mixed = jnp.einsum('hijk,ikhd->ijhd', weights.astype(jnp.float32), values.astype(jnp.float32))
        attended = mixed / total.transpose(1, 2, 0)[..., None]
        gated = (gate_part * attended.reshape(group_rows, TOKENS, C)).astype(jnp.bfloat16)
        return jnp.dot(gated, w_out, preferred_element_type=jnp.float32) + out_shift
    result = lax.map(one_block, (query_blocks, keyval_blocks, gate_blocks))
    return result.reshape(TOKENS, TOKENS, C)
```

```python
import functools

import jax
import jax.numpy as jnp
from jax import lax
from jax.experimental import pallas as pl
from jax.experimental.pallas import tpu as pltpu
from jax.sharding import PartitionSpec as P

HEADS = 4
HEAD_DIM = 32
MASKED = -1000000000.0
ROWS_PER_LN_STEP = 8
ROWS_PER_STEP = 4

VMEM = pltpu.VMEM
NT = (((1,), (1,)), ((), ()))


def chunk_sizes(count):
    half = count // 2
    if count % 2 or half % ROWS_PER_LN_STEP:
        return (count,)
    return (half, count - half)


def norm_kernel(sizes, x_ref, mask_ref, gain_ref, shift_ref, w_ref, *refs):
    outs, bias_ref, w_scr = refs[:-2], refs[-2], refs[-1]
    width = x_ref.shape[1]
    lanes = ROWS_PER_LN_STEP * width
    w = w_ref[...]
    hi = w.astype(jnp.bfloat16).astype(jnp.float32)
    mid = (w - hi).astype(jnp.bfloat16).astype(jnp.float32)
    low = w - hi - mid
    w_scr[...] = jnp.zeros_like(w_scr)
    w_scr[0:HEADS, :] = hi
    w_scr[8 : 8 + HEADS, :] = mid
    w_scr[16 : 16 + HEADS, :] = low
    w3 = w_scr[...].astype(jnp.bfloat16)
    spread = (
        lax.broadcasted_iota(jnp.int32, (width, lanes), 1) % width
        == lax.broadcasted_iota(jnp.int32, (width, lanes), 0)
    ).astype(jnp.float32)
    usable = jnp.dot(
        jnp.broadcast_to(mask_ref[...].astype(jnp.float32), (8, width)).astype(jnp.bfloat16),
        spread.astype(jnp.bfloat16),
        preferred_element_type=jnp.float32,
    )
    gain, shift = gain_ref[...], shift_ref[...]
    at = 0
    for out, size in zip(outs, sizes, strict=True):
        for step in range(size // ROWS_PER_LN_STEP):
            x = x_ref[at : at + ROWS_PER_LN_STEP].reshape(lanes, x_ref.shape[2])
            centred = x - jnp.mean(x, axis=-1, keepdims=True)
            var = jnp.mean(centred * centred, axis=-1, keepdims=True)
            normed = (centred * lax.rsqrt(var + 1e-05) * gain + shift).astype(jnp.bfloat16)
            out[step * ROWS_PER_LN_STEP : (step + 1) * ROWS_PER_LN_STEP] = normed.reshape(
                ROWS_PER_LN_STEP, width, x_ref.shape[2]
            )
            parts = lax.dot_general(w3, normed, NT, preferred_element_type=jnp.float32)
            bias = parts[0:8] + parts[8:16] + parts[16:24]
            bias = jnp.where(usable > 0.5, bias, MASKED)
            bias_ref[:, at * width : at * width + lanes] = bias[0:HEADS]
            at += ROWS_PER_LN_STEP


def attend_kernel(blocks, *refs):
    x_refs = refs[:blocks]
    bias_ref, wq_ref, wkv_ref, wg_ref, gshift_ref, wout_ref, oshift_ref = refs[blocks : blocks + 7]
    out_ref = refs[-1]
    rows, width, chans = x_refs[0].shape
    keys_n = blocks * width
    own = x_refs[0][...].reshape(rows * width, chans)
    every = jnp.concatenate([x[...] for x in x_refs], axis=1).reshape(rows * keys_n, chans)
    queries = (
        jnp.dot(own, wq_ref[...], preferred_element_type=jnp.float32) * HEAD_DIM ** (-0.5)
    ).astype(jnp.bfloat16)
    gates = jax.nn.sigmoid(
        jnp.dot(own, wg_ref[...], preferred_element_type=jnp.float32) + gshift_ref[...]
    )
    keyvals = jnp.dot(every, wkv_ref[...], preferred_element_type=jnp.float32).astype(jnp.bfloat16)
    head_of_lane = lax.broadcasted_iota(jnp.int32, (width, chans), 1) // HEAD_DIM
    ones = jnp.ones((keys_n, chans), jnp.bfloat16)
    bias = bias_ref[...]
    gated = []
    for i in range(rows):
        query = queries[i * width : (i + 1) * width]
        by_head = jnp.concatenate(
            [jnp.where(head_of_lane == h, query, jnp.zeros_like(query)) for h in range(HEADS)], axis=0
        )
        key = keyvals[i * keys_n : (i + 1) * keys_n, :chans]
        value = keyvals[i * keys_n : (i + 1) * keys_n, chans:]
        scores = lax.dot_general(by_head, key, NT, preferred_element_type=jnp.float32) + bias
        expo = jnp.exp(scores - jnp.max(scores, axis=-1, keepdims=True))
        mixed = jnp.dot(
            expo.astype(jnp.bfloat16),
            jnp.concatenate([value, ones], axis=1),
            preferred_element_type=jnp.float32,
        )
        top, total = mixed[0:width, :chans], mixed[0:width, chans:]
        for h in range(1, HEADS):
            part = mixed[h * width : (h + 1) * width]
            top = jnp.where(head_of_lane == h, part[:, :chans], top)
            total = jnp.where(head_of_lane == h, part[:, chans:], total)
        gated.append((gates[i * width : (i + 1) * width] * (top / total)).astype(jnp.bfloat16))
    update = (
        jnp.dot(jnp.concatenate(gated, axis=0), wout_ref[...], preferred_element_type=jnp.float32)
        + oshift_ref[...]
    )
    out_ref[...] = update.reshape(rows, width, chans)


def whole(array):
    return pl.BlockSpec(array.shape, lambda *_: (0,) * array.ndim)


def on_device(
    n_rows,
    n_cols,
    pair_rep,
    token_mask,
    norm_gain,
    norm_shift,
    w_query,
    w_keyval,
    w_gate,
    gate_shift,
    w_bias,
    w_out,
    out_shift,
):
    own_rows, width, chans = pair_rep.shape
    sizes = chunk_sizes(own_rows)
    heads = w_bias.shape[1]
    row_vec = lambda v: v.reshape(1, -1)
    *normed, bias_own = pl.pallas_call(
        functools.partial(norm_kernel, sizes),
        out_shape=[jax.ShapeDtypeStruct((s, width, chans), jnp.bfloat16) for s in sizes]
        + [jax.ShapeDtypeStruct((heads, own_rows * width), jnp.float32)],
        scratch_shapes=[VMEM((24, chans), jnp.float32)],
        name="norm",
    )(pair_rep, row_vec(token_mask), row_vec(norm_gain), row_vec(norm_shift), w_bias.T)

    offsets = [0]
    hops = []
    step = n_rows // 2
    while step:
        hops.append(step)
        offsets += [o ^ step for o in offsets]
        step //= 2

    def gather(part):
        held = [part]
        for hop in hops:
            perm = [(r, r ^ hop) for r in range(n_rows)]
            held += [lax.ppermute(b, "rows", perm) for b in held]
        return held

    gathered = [gather(part) for part in normed]

    r_at, c_at = lax.axis_index("rows"), lax.axis_index("cols")
    if n_rows == n_cols:
        got = []
        for s in range(n_rows):
            perm = [
                (r * n_cols + c, c * n_cols + (r ^ c ^ s)) for r in range(n_rows) for c in range(n_cols)
            ]
            got.append(lax.ppermute(bias_own, ("rows", "cols"), perm))
        slots = []
        for o in offsets:
            slot = got[o]
            for c in range(1, n_cols):
                slot = jnp.where(c_at == c, got[o ^ c], slot)
            slots.append(slot.reshape(heads, width, width))
    else:
        block = lax.all_gather(bias_own.reshape(heads, own_rows, width), "cols", axis=1, tiled=True)
        block = block.reshape(heads, n_rows, width, width)
        block = lax.all_to_all(block, "rows", split_axis=1, concat_axis=1, tiled=True)
        slots = [lax.dynamic_index_in_dim(block, r_at ^ o, 1, keepdims=False) for o in offsets]
    bias = jnp.concatenate(slots, axis=2).reshape(heads * width, n_rows * width)

    small = (
        bias, w_query, w_keyval, w_gate, row_vec(gate_shift), w_out, row_vec(out_shift)
    )
    update = None
    at = 0
    for size, blocks in zip(sizes, gathered, strict=True):
        first = at // ROWS_PER_STEP
        operands = (*blocks, *small)
        in_specs = [
            pl.BlockSpec((ROWS_PER_STEP, width, chans), lambda s: (s, 0, 0)) for _ in blocks
        ] + [whole(a) for a in small]
        aliases = {}
        if update is not None:
            aliases = {len(operands): 0}
            operands += (update,)
            in_specs.append(pl.BlockSpec(memory_space=pl.ANY))
        update = pl.pallas_call(
            functools.partial(attend_kernel, len(blocks)),
            grid=(size // ROWS_PER_STEP,),
            in_specs=in_specs,
            out_specs=pl.BlockSpec((ROWS_PER_STEP, width, chans), lambda s, first=first: (first + s, 0, 0)),
            out_shape=jax.ShapeDtypeStruct(pair_rep.shape, jnp.float32),
            input_output_aliases=aliases,
            name="attend",
        )(*operands)
        at += size
    return update


def solution(mesh):
    return jax.shard_map(
        functools.partial(on_device, mesh.shape["rows"], mesh.shape["cols"]),
        mesh=mesh,
        in_specs=(
            P(("groups", "cols"), "rows", None),
            P(("groups", "rows")),
            P(),
            P(),
            P(),
            P(),
            P(),
            P(),
            P(),
            P(),
            P(),
        ),
        out_specs=P(("groups", "cols"), "rows", None),
        check_vma=False,
    )
```

```python
import functools

import jax
import jax.numpy as jnp
from jax import lax
from jax.experimental import pallas as pl
from jax.experimental.pallas import tpu as pltpu
from jax.sharding import PartitionSpec as P

HEADS = 4
HEAD_DIM = 32
MASKED = -1000000000.0
ROWS_PER_LN_STEP = 8

VMEM = pltpu.VMEM
NT = (((1,), (1,)), ((), ()))


def largest_divisor(count, limit):
    return max(d for d in range(1, min(count, limit) + 1) if count % d == 0)


def chunk_sizes(count):
    half = count // 2
    if count % 2 or half % ROWS_PER_LN_STEP:
        return (count,)
    return (half, count - half)


def norm_kernel(sizes, x_ref, mask_ref, gain_ref, shift_ref, w_ref, *refs):
    outs, bias_ref, w_scr = refs[:-2], refs[-2], refs[-1]
    width = x_ref.shape[1]
    lanes = ROWS_PER_LN_STEP * width
    w = w_ref[...]
    hi = w.astype(jnp.bfloat16).astype(jnp.float32)
    mid = (w - hi).astype(jnp.bfloat16).astype(jnp.float32)
    low = w - hi - mid
    w_scr[...] = jnp.zeros_like(w_scr)
    w_scr[0:HEADS, :] = hi
    w_scr[8 : 8 + HEADS, :] = mid
    w_scr[16 : 16 + HEADS, :] = low
    w3 = w_scr[...].astype(jnp.bfloat16)
    spread = (
        lax.broadcasted_iota(jnp.int32, (width, lanes), 1) % width
        == lax.broadcasted_iota(jnp.int32, (width, lanes), 0)
    ).astype(jnp.float32)
    usable = jnp.dot(
        jnp.broadcast_to(mask_ref[...].astype(jnp.float32), (8, width)).astype(jnp.bfloat16),
        spread.astype(jnp.bfloat16),
        preferred_element_type=jnp.float32,
    )
    gain, shift = gain_ref[...], shift_ref[...]
    at = 0
    for out, size in zip(outs, sizes, strict=True):
        for step in range(size // ROWS_PER_LN_STEP):
            x = x_ref[at : at + ROWS_PER_LN_STEP].reshape(lanes, x_ref.shape[2])
            centred = x - jnp.mean(x, axis=-1, keepdims=True)
            var = jnp.mean(centred * centred, axis=-1, keepdims=True)
            normed = (centred * lax.rsqrt(var + 1e-05) * gain + shift).astype(jnp.bfloat16)
            out[step * ROWS_PER_LN_STEP : (step + 1) * ROWS_PER_LN_STEP] = normed.reshape(
                ROWS_PER_LN_STEP, width, x_ref.shape[2]
            )
            parts = lax.dot_general(w3, normed, NT, preferred_element_type=jnp.float32)
            bias = parts[0:8] + parts[8:16] + parts[16:24]
            bias = jnp.where(usable > 0.5, bias, MASKED)
            bias_ref[:, at * width : at * width + lanes] = bias[0:HEADS]
            at += ROWS_PER_LN_STEP


def attend_kernel(blocks, group, first, *refs):
    x_refs = refs[:blocks]
    bias_ref, wq_ref, wkv_ref, wg_ref, gshift_ref, wout_ref, oshift_ref = refs[blocks : blocks + 7]
    out_ref, k_scr, v_scr, q_scr, g_scr, a_scr, o_scr, sem = refs[-8:]
    rows, width, chans = x_refs[0].shape
    keys_n = blocks * width
    head_of_lane = lax.broadcasted_iota(jnp.int32, (width, chans), 1) // HEAD_DIM
    head_of_query = lax.broadcasted_iota(jnp.int32, (group, width, chans), 2) // HEAD_DIM
    ones = jnp.ones((keys_n, chans), jnp.bfloat16)

    def do_group(start):
        at = pl.ds(start, group)
        own = x_refs[0][at].reshape(group * width, chans)
        queries = (
            (jnp.dot(own, wq_ref[...], preferred_element_type=jnp.float32) * HEAD_DIM ** (-0.5))
            .astype(jnp.bfloat16)
            .reshape(group, width, chans)
        )
        for h in range(HEADS):
            q_scr[at, h * width : (h + 1) * width] = jnp.where(
                head_of_query == h, queries, jnp.zeros_like(queries)
            )
        gates = jnp.dot(own, wg_ref[...], preferred_element_type=jnp.float32) + gshift_ref[...]
        g_scr[at] = jax.nn.sigmoid(gates).reshape(group, width, chans)
        for t, x in enumerate(x_refs):
            keyvals = (
                jnp.dot(
                    x[at].reshape(group * width, chans), wkv_ref[...], preferred_element_type=jnp.float32
                )
                .astype(jnp.bfloat16)
                .reshape(group, width, 2 * chans)
            )
            k_scr[at, t * width : (t + 1) * width] = keyvals[:, :, :chans]
            v_scr[at, t * width : (t + 1) * width] = keyvals[:, :, chans:]
        for u in range(group):
            i = start + u
            scores = (
                lax.dot_general(q_scr[i], k_scr[i], NT, preferred_element_type=jnp.float32)
                + bias_ref[...]
            )
            expo = jnp.exp(scores - jnp.max(scores, axis=-1, keepdims=True))
            mixed = jnp.dot(
                expo.astype(jnp.bfloat16),
                jnp.concatenate([v_scr[i], ones], axis=1),
                preferred_element_type=jnp.float32,
            )
            top, total = mixed[0:width, :chans], mixed[0:width, chans:]
            for h in range(1, HEADS):
                part = mixed[h * width : (h + 1) * width]
                top = jnp.where(head_of_lane == h, part[:, :chans], top)
                total = jnp.where(head_of_lane == h, part[:, chans:], total)
            a_scr[i] = (g_scr[i] * (top / total)).astype(jnp.bfloat16)
        update = (
            jnp.dot(
                a_scr[at].reshape(group * width, chans), wout_ref[...], preferred_element_type=jnp.float32
            )
            + oshift_ref[...]
        )
        o_scr[at] = update.reshape(group, width, chans)

    if rows == group:
        do_group(0)
    else:
        lax.fori_loop(0, rows // group, lambda step, _: do_group(step * group) or 0, 0)
    copy = pltpu.make_async_copy(o_scr, out_ref.at[pl.ds(first, rows)], sem)
    copy.start()
    copy.wait()


def whole(array):
    return pl.BlockSpec(array.shape, lambda *_: (0,) * array.ndim)


def on_device(
    n_rows,
    n_cols,
    pair_rep,
    token_mask,
    norm_gain,
    norm_shift,
    w_query,
    w_keyval,
    w_gate,
    gate_shift,
    w_bias,
    w_out,
    out_shift,
):
    own_rows, width, chans = pair_rep.shape
    sizes = chunk_sizes(own_rows)
    heads = w_bias.shape[1]
    row_vec = lambda v: v.reshape(1, -1)
    *normed, bias_own = pl.pallas_call(
        functools.partial(norm_kernel, sizes),
        out_shape=[jax.ShapeDtypeStruct((s, width, chans), jnp.bfloat16) for s in sizes]
        + [jax.ShapeDtypeStruct((heads, own_rows * width), jnp.float32)],
        scratch_shapes=[VMEM((24, chans), jnp.float32)],
        name="norm",
    )(pair_rep, row_vec(token_mask), row_vec(norm_gain), row_vec(norm_shift), w_bias.T)

    offsets = [0]
    hops = []
    step = n_rows // 2
    while step:
        hops.append(step)
        offsets += [o ^ step for o in offsets]
        step //= 2

    def gather(part):
        held = [part]
        for hop in hops:
            perm = [(r, r ^ hop) for r in range(n_rows)]
            held += [lax.ppermute(b, "rows", perm) for b in held]
        return held

    gathered = [gather(part) for part in normed]

    r_at, c_at = lax.axis_index("rows"), lax.axis_index("cols")
    if n_rows == n_cols and n_rows & (n_rows - 1) == 0:
        held = [bias_own]
        for hop in [1 << k for k in range(n_cols.bit_length() - 1)]:
            perm = [(c, c ^ hop) for c in range(n_cols)]
            held += [lax.ppermute(b, "cols", perm) for b in held]
        at_both = r_at ^ c_at
        slots = []
        for o in offsets:
            slot = held[o]
            for v in range(1, n_cols):
                slot = jnp.where(at_both == v, held[o ^ v], slot)
            if o:
                slot = lax.ppermute(slot, "rows", [(r, r ^ o) for r in range(n_rows)])
            slots.append(slot.reshape(heads, width, width))
    else:
        block = lax.all_gather(bias_own.reshape(heads, own_rows, width), "cols", axis=1, tiled=True)
        block = block.reshape(heads, n_rows, width, width)
        block = lax.all_to_all(block, "rows", split_axis=1, concat_axis=1, tiled=True)
        slots = [lax.dynamic_index_in_dim(block, r_at ^ o, 1, keepdims=False) for o in offsets]
    bias = jnp.concatenate(slots, axis=2).reshape(heads * width, n_rows * width)

    small = (bias, w_query, w_keyval, w_gate, row_vec(gate_shift), w_out, row_vec(out_shift))
    in_vmem, in_place = pl.BlockSpec(memory_space=pltpu.VMEM), pl.BlockSpec(memory_space=pl.ANY)
    update = None
    at = 0
    for size, blocks in zip(sizes, gathered, strict=True):
        operands = (*blocks, *small)
        in_specs = [in_vmem] * len(operands)
        aliases = {}
        if update is not None:
            aliases = {len(operands): 0}
            operands += (update,)
            in_specs.append(in_place)
        keys_n = width * len(blocks)
        group = largest_divisor(size, max(1, 96 // len(blocks)))
        update = pl.pallas_call(
            functools.partial(attend_kernel, len(blocks), group, at),
            in_specs=in_specs,
            out_specs=in_place,
            out_shape=jax.ShapeDtypeStruct(pair_rep.shape, jnp.float32),
            scratch_shapes=[
                VMEM((size, keys_n, chans), jnp.bfloat16),
                VMEM((size, keys_n, chans), jnp.bfloat16),
                VMEM((size, heads * width, chans), jnp.bfloat16),
                VMEM((size, width, chans), jnp.float32),
                VMEM((size, width, chans), jnp.bfloat16),
                VMEM((size, width, chans), jnp.float32),
                pltpu.SemaphoreType.DMA,
            ],
            input_output_aliases=aliases,
            name="attend",
        )(*operands)
        at += size
    return update


def solution(mesh):
    return jax.shard_map(
        functools.partial(on_device, mesh.shape["rows"], mesh.shape["cols"]),
        mesh=mesh,
        in_specs=(
            P(("groups", "cols"), "rows", None),
            P(("groups", "rows")),
            P(),
            P(),
            P(),
            P(),
            P(),
            P(),
            P(),
            P(),
            P(),
        ),
        out_specs=P(("groups", "cols"), "rows", None),
        check_vma=False,
    )
```
